128 devices in a mesh: row: 8 (over x, core), col: 16 (over z, y).
Axes of the slice: x: 4, y: 4, z: 4, core: 2. Of those that a mesh axis runs over, the one named last changes fastest.
Arguments:
- dinv_root: bfloat16 [16384, 16384], P('row', 'col'), may hold values from -0.03125 to 0.03125
- rhs_root: bfloat16 [16384, 384], P('col'), may hold values from -6 to 6
- dinv_mid: bfloat16 [32768, 8192], P('row', 'col'), may hold values from -0.046875 to 0.046875
- coup_mid: bfloat16 [32768, 8192], P('row', 'col'), may hold values from -0.0625 to 0.0625
- rhs_mid: bfloat16 [4, 8192, 384], P(None, 'col'), may hold values from -6 to 6
- dinv_leaf: bfloat16 [16, 4096, 4096], P('col', None, 'row'), may hold values from -0.0625 to 0.0625
- coup_leaf: bfloat16 [16, 6144, 4096], P('col', 'row'), may hold values from -0.109375 to 0.109375
- rhs_leaf: bfloat16 [16, 4096, 384], P('col', 'row'), may hold values from -6 to 6
- bounds_mid: int32 [4, 64], replicated, may hold values from 0 to 127, as said below
- bounds_leaf: int32 [16, 48], replicated, may hold values from 0 to 191, as said below
- parents: int32 [16], replicated, may hold values from 0 to 3, as said below
Outputs:
- root_values: bfloat16 [16384, 384], P(('row', 'col'))
- mid_values: bfloat16 [32768, 384], P(('row', 'col'))
- leaf_values: bfloat16 [16, 4096, 384], P('col', 'row')
The draws below stay inside these ranges and needn't reach their ends.
Inputs may be any that keep to these rules, and one draw needn't show every extreme that they name: `bounds_mid`: each row holds 64 distinct root block numbers; every root block appears in some row. `parents`: each mid front is the parent of exactly 4 leaf fronts. `bounds_leaf`: each row holds 48 distinct values. Every row names the same number of root blocks; the leaf fronts of one parent together name each block of that parent's separator exactly once, each naming 8192 / 128 / 4 of them.
All inputs are finite; a program needn't handle non-finite values.
Results may differ from the reference program's by a relative error of at most 0.0065.
Values may be sent and summed in bfloat16 or wider, within the bound.
A program may use at most 128 MiB of HBM per device.

```python
import jax
import jax.numpy as jnp
from jax import lax

N0 = 16384
N1 = 8192
N2 = 4096
B1 = 8192
B2 = 6144
BLOCK = 128
RHS = 384
F1 = 4
F2 = 16


def draw_bounds_mid(key, part):
    root_total = N0 // BLOCK
    list_len = B1 // BLOCK
    root_order = jax.random.permutation(jax.random.fold_in(key, 3), root_total).astype(jnp.int32)
    stride = root_total // F1

    def front_list(front_id):
        positions = (front_id * stride + jnp.arange(list_len, dtype=jnp.int32)) % root_total
        shuffle = jax.random.permutation(jax.random.fold_in(key, 200 + front_id), list_len)
        return root_order[positions][shuffle]
    return jax.vmap(front_list)(jnp.arange(F1, dtype=jnp.int32)).astype(jnp.int32)


def leaf_tables(key):
    base_key = jax.random.fold_in(key, 11)
    slot_order = jax.random.permutation(jax.random.fold_in(base_key, 1), F2).astype(jnp.int32)
    fan_out = F2 // F1
    parent_ids = slot_order // fan_out
    ordinal = slot_order % fan_out
    parent_total = N1 // BLOCK
    per_child = parent_total // fan_out
    root_total = N0 // BLOCK
    root_take = B2 // BLOCK - per_child
    root_order = jax.random.permutation(jax.random.fold_in(base_key, 2), root_total).astype(jnp.int32)
    stride = root_total // F2

    def parent_deal(parent_id):
        return jax.random.permutation(jax.random.fold_in(base_key, 300 + parent_id), parent_total).astype(jnp.int32)
    parent_orders = jax.vmap(parent_deal)(jnp.arange(F1, dtype=jnp.int32))

    def child_list(slot_id):
        positions = (slot_id * stride + jnp.arange(root_take, dtype=jnp.int32)) % root_total
        root_pick = root_order[positions]
        dealt = parent_orders[parent_ids[slot_id]]
        own_part = root_total + dealt[ordinal[slot_id] * per_child + jnp.arange(per_child, dtype=jnp.int32)]
        entries = jnp.concatenate([root_pick, own_part])
        shuffle = jax.random.permutation(jax.random.fold_in(base_key, 100 + slot_id), B2 // BLOCK)
        return entries[shuffle]
    all_lists = jax.vmap(child_list)(jnp.arange(F2, dtype=jnp.int32))
    return (parent_ids.astype(jnp.int32), all_lists.astype(jnp.int32))


def draw_bounds_leaf(key, part):
    return leaf_tables(key)[1]


def draw_parents(key, part):
    return leaf_tables(key)[0]


def strengthened(drawn, stream_key, source, target, shards_of, factor):
    def block_of(position):
        return (jnp.arange(drawn.shape[position]) // (drawn.shape[position] // shards_of)).reshape((-1,) + (1,) * (drawn.ndim - 1 - position))

    one_side = jax.random.permutation(stream_key, shards_of)[block_of(target)]
    second = (block_of(target) + shards_of // 2) % shards_of
    return jnp.where((block_of(source) == one_side) | (block_of(source) == second), factor * drawn, drawn)


def levels(own_key, dims, shards, low, high):
    factor_of = 1.0
    for position, shards_of in shards:
        heights = jax.random.uniform(jax.random.fold_in(jax.random.fold_in(own_key, 6), position), (shards_of,), jnp.float32, low / len(shards), high / len(shards))
        factor_of = factor_of * jnp.repeat(jnp.exp(heights), dims[position] // shards_of).reshape((-1,) + (1,) * (len(dims) - 1 - position))
    return factor_of


def scatter_about(key, extent, deviation, reach, shards=(), kind=jnp.bfloat16):
    values = jax.random.normal(key, extent, jnp.float32) * deviation
    if len(shards) > 0:
        values = levels(key, extent, shards, -0.22, 0.18) * values
    return jnp.clip(values, min=-reach, max=reach).astype(kind)


def bell_draw_with(key, shape, width, reach, cuts, heavy, kind=jnp.bfloat16):
    drawn = width * jax.random.normal(key, shape, jnp.float32)
    if cuts:
        drawn = drawn * levels(key, shape, cuts, -0.22, 0.18)
    return jnp.clip(strengthened(drawn, jax.random.fold_in(key, 3), *heavy), -reach, reach).astype(kind)


def setup_inputs(seed: int = 0) -> dict:
    keys = jax.random.split(jax.random.key(seed), 12)
    return {
        "dinv_root": bell_draw_with(keys[0], (N0, N0), (4 * N0) ** -0.5, 0.03125, ((0, 8), (1, 16)), (1, 0, 16, 2.0)),
        "rhs_root": scatter_about(keys[1], (N0, RHS), 1.0, 6.0, ((0, 16),)),
        "dinv_mid": bell_draw_with(keys[2], (F1 * N1, N1), (4 * N1) ** -0.5, 0.046875, ((0, 8), (1, 16)), (1, 0, 16, 2.0)),
        "coup_mid": scatter_about(keys[3], (F1 * B1, N1), B1 ** -0.5, 0.0625, ((0, 8), (1, 16))),
        "rhs_mid": scatter_about(keys[4], (F1, N1, RHS), 1.0, 6.0, ((1, 16),)),
        "dinv_leaf": bell_draw_with(keys[5], (F2, N2, N2), (4 * N2) ** -0.5, 0.0625, ((0, 16), (2, 8)), (2, 1, 8, 2.0)),
        "coup_leaf": bell_draw_with(keys[6], (F2, B2, N2), B2 ** -0.5, 0.109375, ((0, 16), (1, 8)), (1, 2, 8, 2.0)),
        "rhs_leaf": scatter_about(keys[7], (F2, N2, RHS), 1.0, 6.0, ((0, 16), (1, 8))),
        "bounds_mid": draw_bounds_mid(jax.random.fold_in(keys[11], 71), 0),
        "bounds_leaf": draw_bounds_leaf(jax.random.fold_in(keys[11], 71), 0),
        "parents": draw_parents(jax.random.fold_in(keys[11], 71), 0),
    }


def reference(dinv_root, rhs_root, dinv_mid, coup_mid, rhs_mid, dinv_leaf, coup_leaf, rhs_leaf, bounds_mid, bounds_leaf, parents):
    rhs_width = rhs_root.shape[1]
    root_values = jnp.dot(dinv_root, rhs_root, preferred_element_type=jnp.float32).astype(jnp.bfloat16)
    root_blocks = root_values.reshape(N0 // BLOCK, BLOCK, rhs_width)

    def mid_front(front_id):
        boundary = root_blocks[bounds_mid[front_id]].reshape(B1, rhs_width)
        coupling = lax.dynamic_slice_in_dim(coup_mid, front_id * B1, B1, 0)
        terms = jnp.dot(coupling.T, boundary, preferred_element_type=jnp.float32)
        shifted = (rhs_mid[front_id].astype(jnp.float32) - terms).astype(jnp.bfloat16)
        inverse = lax.dynamic_slice_in_dim(dinv_mid, front_id * N1, N1, 0)
        return jnp.dot(inverse, shifted, preferred_element_type=jnp.float32).astype(jnp.bfloat16)

    mid_stack = lax.map(mid_front, jnp.arange(F1, dtype=jnp.int32))
    mid_values = mid_stack.reshape(F1 * N1, rhs_width)

    def leaf_front(slot_id):
        parent_blocks = mid_stack[parents[slot_id]].reshape(N1 // BLOCK, BLOCK, rhs_width)
        sources = jnp.concatenate([root_blocks, parent_blocks], axis=0)
        boundary = sources[bounds_leaf[slot_id]].reshape(B2, rhs_width)
        terms = jnp.dot(coup_leaf[slot_id].T, boundary, preferred_element_type=jnp.float32)
        shifted = (rhs_leaf[slot_id].astype(jnp.float32) - terms).astype(jnp.bfloat16)
        return jnp.dot(dinv_leaf[slot_id], shifted, preferred_element_type=jnp.float32).astype(jnp.bfloat16)

    leaf_values = lax.map(leaf_front, jnp.arange(F2, dtype=jnp.int32))
    return root_values, mid_values, leaf_values
```

```python
import functools

import jax
import jax.numpy as jnp
from jax import lax
from jax.experimental import pallas as pl
from jax.experimental.pallas import tpu as pltpu
from jax.sharding import PartitionSpec as P

MESH = pl.DeviceIdType.MESH
BF = jnp.bfloat16
F32 = jnp.float32
BLOCK = 128
NT = (((1,), (1,)), ((), ()))


def position():
    row, col = lax.axis_index("row"), lax.axis_index("col")
    return row, col, lax.div(row, 2), lax.rem(row, 2), lax.div(col, 4), lax.rem(col, 4)


def ring(p, d):
    return lax.rem(p + d, 4)


class Links:
    def __init__(self, send, recv):
        self.send, self.recv, self.made = send, recv, []

    def __call__(self, src, dst, device):
        i = len(self.made)
        copy = pltpu.make_async_remote_copy(
            src_ref=src,
            dst_ref=dst,
            send_sem=self.send.at[i],
            recv_sem=self.recv.at[i],
            device_id=device,
            device_id_type=MESH,
        )
        copy.start()
        self.made.append(copy)
        return copy

    def drain(self):
        for copy in self.made:
            copy.wait_send()


def greet(peers):
    barrier = pltpu.get_barrier_semaphore()
    for peer in peers:
        pl.semaphore_signal(barrier, inc=1, device_id=peer, device_id_type=MESH)
    pl.semaphore_wait(barrier, len(peers))


def ring_sum(links, value, up, down, s, rf, rn, p):
    s[1, 0] = value(2, 0).astype(BF)
    far_up = links(s.at[1, 0], rf.at[0], up)
    s[1, 1] = value(2, 1).astype(BF)
    far_down = links(s.at[1, 1], rf.at[1], down)
    s[0, 1] = value(1, 1).astype(BF)
    last = [links(s.at[0, 1], rn.at[0, 1], up)]
    s[2, 0] = value(3, 0).astype(BF)
    last.append(links(s.at[2, 0], rn.at[1, 0], down))
    p[0] = value(1, 0)
    p[1] = value(3, 1)
    far_up.wait_recv()
    s[0, 0] = (p[0] + rf[0].astype(F32)).astype(BF)
    last.append(links(s.at[0, 0], rn.at[0, 0], up))
    far_down.wait_recv()
    s[2, 1] = (p[1] + rf[1].astype(F32)).astype(BF)
    last.append(links(s.at[2, 1], rn.at[1, 1], down))
    p[2] = value(0, 0)
    p[3] = value(0, 1)
    for copy in last:
        copy.wait_recv()
    return [p[2 + h] + rn[0, h].astype(F32) + rn[1, h].astype(F32) for h in range(2)]


def root_kernel(
    bm, bl, root_t, mid_t, w_hbm, c_hbm,
    out_root, out_shift, out_side,
    w, c, ra, s1, rf1, rn1, p1, y1, s2, rf2, rn2, p2, bt, ex, exr,
    local, send, recv,
):
    row, col, x, k, z, y = position()
    a, b = k * z + (1 - k) * y, k * y + (1 - k) * z

    def chip(a_, b_):
        return k * (4 * a_ + b_) + (1 - k) * (4 * b_ + a_)

    load_w = pltpu.make_async_copy(w_hbm, w, local.at[0])
    load_c = pltpu.make_async_copy(c_hbm, c, local.at[1])
    load_w.start()
    load_c.start()
    along = {
        "x": lambda d: (2 * ring(x, d) + k, col),
        "y": lambda d: (row, 4 * z + ring(y, d)),
        "z": lambda d: (row, 4 * ring(z, d) + y),
    }
    partner = (2 * x + 1 - k, col)
    greet([along[axis](d) for axis in "xyz" for d in (1, 3)] + [partner])
    links = Links(send, recv)
    load_w.wait()

    def root_term(d, h):
        ids = [chip(ring(a, d), 2 * h + j) for j in range(2)]
        rows = jnp.concatenate(
            [w[pl.ds(pl.multiple_of(i * BLOCK, BLOCK), BLOCK), :] for i in ids], axis=0
        )
        return lax.dot_general(root_t[...], rows, NT, preferred_element_type=F32)

    halves = ring_sum(
        links, root_term, (row, chip(ring(a, 1), b)), (row, chip(ring(a, 3), b)), s1, rf1, rn1, p1
    )
    for h in range(2):
        for j in range(2):
            y1[2 * h + j] = halves[h][:, j * BLOCK : (j + 1) * BLOCK]
    tall = y1.shape[1] // 2
    halves = ring_sum(
        links,
        lambda d, h: y1[ring(b, d), h * tall : (h + 1) * tall, :],
        (row, chip(a, ring(b, 1))),
        (row, chip(a, ring(b, 3))),
        s2, rf2, rn2, p2,
    )
    for h in range(2):
        half = halves[h].astype(BF)
        ra[x, k, z, y, h * tall : (h + 1) * tall, :] = half
        out_root[h * tall : (h + 1) * tall, :] = half

    third = ra.shape[4] // 3
    here = {"x": x, "y": y, "z": z}

    def view(part, done, axis, at, half):
        index = []
        lead = True
        split = half is not None
        for name in ("x", "k", "z", "y"):
            if name == "k":
                index.append(k)
            elif name == axis:
                index.append(at)
            elif name in done:
                if split and lead:
                    index.append(pl.ds(2 * half, 2))
                else:
                    index.append(slice(None))
                lead = False
            else:
                index.append(here[name])
        if split and not done:
            index.append(pl.ds(part * third + half * (third // 2), third // 2))
        else:
            index.append(pl.ds(part * third, third))
        return ra.at[tuple(index)]

    orders = ("xyz", "yzx", "zxy")
    shared = []

    def share(ref):
        shared.append(links(ref, ref, partner))

    for phase in range(3):
        state = []
        for part, order in enumerate(orders):
            axis, done, at = order[phase], order[:phase], here[order[phase]]
            own = view(part, done, axis, at, None)
            state.append((links(own, own, along[axis](1)), links(own, own, along[axis](3))))
            if phase == 2:
                share(own)
        onward = []
        for part, order in enumerate(orders):
            axis, done, at = order[phase], order[:phase], here[order[phase]]
            state[part][0].wait_recv()
            got = view(part, done, axis, ring(at, 3), 0)
            first = links(got, got, along[axis](1))
            state[part][1].wait_recv()
            got = view(part, done, axis, ring(at, 1), 1)
            onward.append((first, links(got, got, along[axis](3))))
            if phase == 2:
                share(view(part, done, axis, ring(at, 3), None))
                share(view(part, done, axis, ring(at, 1), None))
        for part, order in enumerate(orders):
            axis, done, at = order[phase], order[:phase], here[order[phase]]
            for half in range(2):
                onward[part][half].wait_recv()
                if phase == 2:
                    share(view(part, done, axis, ring(at, 2), half))
    for copy in shared:
        copy.wait_recv()

    def root_block(v):
        return ra[lax.div(v, 32), lax.rem(lax.div(v, 16), 2), lax.rem(lax.div(v, 4), 4), lax.rem(v, 4)]

    load_c.wait()
    count = bm.shape[1] // 2
    group = bt.shape[1] // BLOCK
    for g in range(count // group):
        for j in range(group):
            bt[:, j * BLOCK : (j + 1) * BLOCK] = root_block(bm[x, k * count + g * group + j])
        rows = group * BLOCK
        term = jnp.dot(bt[...], c[g * rows : (g + 1) * rows, :], preferred_element_type=F32)
        if g == 0:
            ex[...] = term
        else:
            ex[...] += term
    swap = links(ex, exr, partner)
    slots = out_side.shape[0]
    for i in range(slots):
        out_side[i] = root_block(jnp.minimum(bl[col, row * slots + i], 127))
    swap.wait_recv()
    out_shift[...] = (mid_t[...].astype(F32) - (ex[...] + exr[...])).astype(BF)
    links.drain()


def mid_kernel(
    bl, parents, shift, side, w_hbm,
    out_mid, out_bound,
    w, s1, rf1, rn1, p1, y1, s2, rf2, rn2, p2, m4, r, ts, t, u, bb,
    local, send, recv,
):
    row, col, x, k, z, y = position()
    a, b = k * z + (1 - k) * y, k * y + (1 - k) * z

    def chip(a_, b_):
        return k * (4 * a_ + b_) + (1 - k) * (4 * b_ + a_)

    load_w = pltpu.make_async_copy(w_hbm, w, local.at[0])
    load_w.start()
    offsets = [(i, j) for i in (2, 1, 3, 0) for j in (2, 1, 3, 0) if (i, j) != (0, 0)]

    def plane(dz, dy):
        return 4 * ring(z, dz) + ring(y, dy)

    partner = (2 * x + 1 - k, col)
    greet(
        [(row, plane(*o)) for o in offsets]
        + [(2 * ring(x, d) + k, col) for d in (1, 2, 3)]
        + [partner]
    )
    links = Links(send, recv)
    load_w.wait()
    wide = 2 * BLOCK

    def mid_term(d, h):
        ids = [chip(ring(a, d), 2 * h + j) for j in range(2)]
        rows = jnp.concatenate(
            [w[pl.ds(pl.multiple_of(i * wide, wide), wide), :] for i in ids], axis=0
        )
        return lax.dot_general(shift[...], rows, NT, preferred_element_type=F32)

    halves = ring_sum(
        links, mid_term, (row, chip(ring(a, 1), b)), (row, chip(ring(a, 3), b)), s1, rf1, rn1, p1
    )
    for h in range(2):
        for j in range(2):
            y1[2 * h + j] = halves[h][:, j * wide : (j + 1) * wide]
    tall = y1.shape[1] // 2
    halves = ring_sum(
        links,
        lambda d, h: y1[ring(b, d), h * tall : (h + 1) * tall, :],
        (row, chip(a, ring(b, 1))),
        (row, chip(a, ring(b, 3))),
        s2, rf2, rn2, p2,
    )
    quarter = tall // 2
    for h in range(2):
        half = halves[h].astype(BF)
        out_mid[h * tall : (h + 1) * tall, :] = half
        for i in range(2):
            for j in range(2):
                m4[2 * h + i, j] = half[
                    i * quarter : (i + 1) * quarter, j * BLOCK : (j + 1) * BLOCK
                ]
    moved = []
    for d in (2, 1, 3):
        q = ring(x, d)
        moved.append(links(m4.at[q], r.at[x], (2 * q + k, col)))
    r[x] = m4[x]
    for copy in moved:
        copy.wait_recv()
    moved = []
    for i, (dz, dy) in enumerate(offsets):
        to = plane(dz, dy)
        ts[i] = r[parents[to]]
        moved.append(links(ts.at[i], t.at[k, col], (row, to)))
    t[k, col] = r[parents[col]]
    shared = [links(t.at[k, col], t.at[k, col], partner)]
    for copy, (dz, dy) in zip(moved, offsets):
        copy.wait_recv()
        got = t.at[k, plane(4 - dz, 4 - dy)]
        shared.append(links(got, got, partner))
    for copy in shared:
        copy.wait_recv()
    slots = side.shape[0]

    def parent_block(v):
        m = jnp.maximum(v - 128, 0)
        return t[lax.div(m, 32), lax.div(lax.rem(m, 32), 2), lax.rem(m, 2)]

    moved = []
    for d in (2, 1, 3):
        q = ring(x, d)
        for i in range(slots):
            u[d - 1, i] = parent_block(bl[col, (2 * q + k) * slots + i])
        moved.append(links(u.at[d - 1], bb.at[x], (2 * q + k, col)))
    for i in range(slots):
        bb[x, i] = parent_block(bl[col, row * slots + i])
    for copy in moved:
        copy.wait_recv()
    for i in range(slots):
        from_root = bl[col, row * slots + i] < 128
        for q in range(4):
            span = slice(q * quarter, (q + 1) * quarter)
            out_bound[span, i * BLOCK : (i + 1) * BLOCK] = jnp.where(
                from_root, side[i, span, :].astype(F32), bb[q, i].astype(F32)
            ).astype(BF)
    links.drain()


def leaf_kernel(
    bound, leaf_t, c_hbm, w_hbm,
    out_leaf,
    c, w, own, sp, rp1, rp2, s1, rf1, rn1, s2, rf2, rn2, p, shift,
    local, send, recv,
):
    row, col, x, k, z, y = position()
    load_c = pltpu.make_async_copy(c_hbm, c, local.at[0])
    load_w = pltpu.make_async_copy(w_hbm, w, local.at[1])
    load_c.start()
    load_w.start()
    partner = (2 * x + 1 - k, col)
    up, down = (2 * ring(x, 1) + k, col), (2 * ring(x, 3) + k, col)
    greet([partner, up, down])
    links = Links(send, recv)
    size = own.shape[2]
    tall = own.shape[1] // 2

    def chunk(q, core):
        return pl.ds(pl.multiple_of((2 * q + core) * size, size), size)

    def scatter(product, rp, stage, s, rf, rn):
        order = [2, 1, 3, 0]
        sent, ready = {}, set()

        def make(d):
            q = ring(x, d)
            sp[stage, d] = product(chunk(q, 1 - k)).astype(BF)
            sent[d] = links(sp.at[stage, d], rp.at[d], partner)
            own[d] = product(chunk(q, k))

        def value(d, h):
            upto = min(order.index(d) + 1, 3)
            for e in order[: upto + 1]:
                if e not in sent:
                    make(e)
            if d not in ready:
                sent[d].wait_recv()
                ready.add(d)
            rows = slice(h * tall, (h + 1) * tall)
            return own[d, rows, :] + rp[d, rows, :].astype(F32)

        return ring_sum(links, value, up, down, s, rf, rn, p)

    load_c.wait()
    halves = scatter(
        lambda span: jnp.dot(bound[...], c[:, span], preferred_element_type=F32),
        rp1, 0, s1, rf1, rn1,
    )
    for h in range(2):
        rows = slice(h * tall, (h + 1) * tall)
        shift[rows, :] = (leaf_t[rows, :].astype(F32) - halves[h]).astype(BF)
    load_w.wait()
    halves = scatter(
        lambda span: lax.dot_general(shift[...], w[span, :], NT, preferred_element_type=F32),
        rp2, 1, s2, rf2, rn2,
    )
    for h in range(2):
        out_leaf[h * tall : (h + 1) * tall, :] = halves[h].astype(BF)
    links.drain()


VM = pl.BlockSpec(memory_space=pltpu.VMEM)
SM = pl.BlockSpec(memory_space=pltpu.SMEM)
ANY = pl.BlockSpec(memory_space=pl.ANY)


def call(kernel, number, in_specs, outs, scratch, copies, args):
    return pl.pallas_call(
        kernel,
        out_shape=tuple(jax.ShapeDtypeStruct(shape, BF) for shape in outs),
        in_specs=in_specs,
        out_specs=(VM,) * len(outs),
        scratch_shapes=[pltpu.VMEM(shape, kind) for shape, kind in scratch]
        + [
            pltpu.SemaphoreType.DMA((2,)),
            pltpu.SemaphoreType.DMA((copies,)),
            pltpu.SemaphoreType.DMA((copies,)),
        ],
        compiler_params=pltpu.CompilerParams(
            collective_id=number, has_side_effects=True, vmem_limit_bytes=58 * 1024 * 1024
        ),
    )(*args)


def ring_scratch(half):
    return [((3, 2) + half, BF), ((2,) + half, BF), ((2, 2) + half, BF), ((4,) + half, F32)]


def shards(
    dinv_root, rhs_root, dinv_mid, coup_mid, rhs_mid, dinv_leaf, coup_leaf, rhs_leaf,
    bounds_mid, bounds_leaf, parents,
):
    front = lax.div(lax.axis_index("row"), 2)
    n = rhs_root.shape[1]
    slots = bounds_leaf.shape[1] // 8
    sep_mid, sep_leaf = rhs_mid.shape[1], rhs_leaf.shape[1]
    root_t = rhs_root.T
    mid_t = lax.dynamic_index_in_dim(rhs_mid, front, 0, keepdims=False).T
    leaf_t = rhs_leaf[0].T
    wide = 2 * BLOCK
    root_out, shift, side = call(
        root_kernel, 0,
        [SM, SM, VM, VM, ANY, ANY],
        [(n, BLOCK), (n, sep_mid), (slots, n, BLOCK)],
        [(dinv_root.shape, BF), (coup_mid.shape, BF), ((4, 2, 4, 4, n, BLOCK), BF)]
        + ring_scratch((n, wide))
        + [((4, n, BLOCK), F32)]
        + ring_scratch((n // 2, BLOCK))
        + [((n, 8 * BLOCK), BF), ((n, sep_mid), F32), ((n, sep_mid), F32)],
        64,
        (bounds_mid, bounds_leaf, root_t, mid_t, dinv_root, coup_mid),
    )
    quarter = n // 4
    mid_out, bound = call(
        mid_kernel, 1,
        [SM, SM, VM, VM, ANY],
        [(n, wide), (n, slots * BLOCK)],
        [(dinv_mid.shape, BF)]
        + ring_scratch((n, 2 * wide))
        + [((4, n, wide), F32)]
        + ring_scratch((n // 2, wide))
        + [
            ((4, 2, quarter, BLOCK), BF),
            ((4, 2, quarter, BLOCK), BF),
            ((15, 2, quarter, BLOCK), BF),
            ((2, 16, 2, quarter, BLOCK), BF),
            ((3, slots, quarter, BLOCK), BF),
            ((4, slots, quarter, BLOCK), BF),
        ],
        64,
        (bounds_leaf, parents, shift, side, dinv_mid),
    )
    (leaf_out,) = call(
        leaf_kernel, 2,
        [VM, VM, ANY, ANY],
        [(n, sep_leaf)],
        [
            (coup_leaf.shape[1:], BF),
            (dinv_leaf.shape[1:], BF),
            ((4, n, sep_leaf), F32),
            ((2, 4, n, sep_leaf), BF),
            ((4, n, sep_leaf), BF),
            ((4, n, sep_leaf), BF),
        ]
        + ring_scratch((n // 2, sep_leaf))[:3]
        + ring_scratch((n // 2, sep_leaf))
        + [((n, sep_leaf), BF)],
        32,
        (bound, leaf_t, coup_leaf[0], dinv_leaf[0]),
    )
    return root_out.T, mid_out.T, leaf_out.T[None]


def solution(mesh):
    return jax.shard_map(
        shards,
        mesh=mesh,
        in_specs=(
            P("row", "col"),
            P("col", None),
            P("row", "col"),
            P("row", "col"),
            P(None, "col", None),
            P("col", None, "row"),
            P("col", "row", None),
            P("col", "row", None),
            P(),
            P(),
            P(),
        ),
        out_specs=(P(("row", "col"), None), P(("row", "col"), None), P("col", "row", None)),
        check_vma=False,
    )
```

```python
import functools

import jax
import jax.numpy as jnp
from jax import lax
from jax.experimental import pallas as pl
from jax.experimental.pallas import tpu as pltpu
from jax.sharding import PartitionSpec as P

MESH = pl.DeviceIdType.MESH
BF = jnp.bfloat16
F32 = jnp.float32
BLOCK = 128
NT = (((1,), (1,)), ((), ()))


def position():
    row, col = lax.axis_index("row"), lax.axis_index("col")
    return row, col, lax.div(row, 2), lax.rem(row, 2), lax.div(col, 4), lax.rem(col, 4)


def ring(p, d):
    return lax.rem(p + d, 4)


class Links:
    def __init__(self, send, recv):
        self.send, self.recv, self.made, self.done = send, recv, [], set()

    def __call__(self, src, dst, device):
        i = len(self.made)
        copy = pltpu.make_async_remote_copy(
            src_ref=src,
            dst_ref=dst,
            send_sem=self.send.at[i],
            recv_sem=self.recv.at[i],
            device_id=device,
            device_id_type=MESH,
        )
        copy.start()
        self.made.append(copy)
        return copy

    def sent(self, copies):
        for copy in copies:
            if id(copy) not in self.done:
                self.done.add(id(copy))
                copy.wait_send()

    def drain(self):
        self.sent(self.made)


def greet(peers):
    barrier = pltpu.get_barrier_semaphore()
    for peer in peers:
        pl.semaphore_signal(barrier, inc=1, device_id=peer, device_id_type=MESH)
    pl.semaphore_wait(barrier, len(peers))


def ring_sum(links, value, prepare, up, down, s, rf, rn, p):
    yield from prepare(2)
    s(1, 0)[...] = value(2, 0).astype(BF)
    far_up = links(s(1, 0), rf.at[0], up)
    s(1, 1)[...] = value(2, 1).astype(BF)
    far_down = links(s(1, 1), rf.at[1], down)
    yield from prepare(1)
    s(0, 1)[...] = value(1, 1).astype(BF)
    last = [links(s(0, 1), rn.at[0, 1], up)]
    yield from prepare(3)
    s(2, 0)[...] = value(3, 0).astype(BF)
    last.append(links(s(2, 0), rn.at[1, 0], down))
    if p is not None:
        for i, term in enumerate(((1, 0), (3, 1), (0, 0), (0, 1))):
            p(i)[...] = value(*term)
    kept = (lambda i, d, h: p(i)[...]) if p is not None else (lambda i, d, h: value(d, h))
    yield
    far_up.wait_recv()
    s(0, 0)[...] = (kept(0, 1, 0) + rf[0].astype(F32)).astype(BF)
    last.append(links(s(0, 0), rn.at[0, 0], up))
    yield
    far_down.wait_recv()
    s(2, 1)[...] = (kept(1, 3, 1) + rf[1].astype(F32)).astype(BF)
    last.append(links(s(2, 1), rn.at[1, 1], down))
    yield from prepare(0)
    yield
    for copy in last:
        copy.wait_recv()
    halves = [
        kept(2 + h, 0, h) + rn[0, h].astype(F32) + rn[1, h].astype(F32) for h in range(2)
    ]
    return halves, last + [far_up, far_down]


def ring_direct(links, value, to, s, rn):
    moved = []
    for d in (2, 1, 3):
        s(d - 1)[...] = value(d).astype(BF)
        moved.append(links(s(d - 1), rn.at[d - 1], to(d)))
    yield
    total = value(0)
    for copy, d in zip(moved, (2, 1, 3)):
        copy.wait_recv()
        total += rn[d - 1].astype(F32)
    return total, moved


def nothing(d):
    return
    yield


def together(programs, lag):
    turn, live = 0, list(enumerate(programs))
    while live:
        for item in list(live):
            if turn >= item[0] * lag:
                try:
                    next(item[1])
                except StopIteration:
                    live.remove(item)
        turn += 1


def kernel(
    groups, lag,
    bm, bl, parents, root_hbm, mid_hbm, leaf_hbm, w_hbm, c_hbm, dm_hbm, cl_hbm, dl_hbm,
    out_root, out_mid, out_leaf,
    root_v, root_t, mid_v, mid_t, leaf_v, leaf_t,
    w, c, dm, cl, ra_0, ra_1, pool, y1, sa, sb,
    rf1r, rn1r, rn2r, rf1m, rn1m, rn2m, exr, shift,
    m4, rq_0, rq_1, ts, t_0, t_1, u, bb, bound, sp, rp1, rp2, rf1l, rn1l, rf2l, rn2l,
    local, send, recv,
):
    row, col, x, k, z, y = position()
    a, b = k * z + (1 - k) * y, k * y + (1 - k) * z
    size = root_t.shape[0] // groups
    wide = 2 * BLOCK

    def chip(a_, b_):
        return k * (4 * a_ + b_) + (1 - k) * (4 * b_ + a_)

    def plane(dz, dy):
        return 4 * ring(z, dz) + ring(y, dy)

    def fetch(source, target, i):
        copy = pltpu.make_async_copy(source, target, local.at[i])
        copy.start()
        return copy

    loads = {"root": [fetch(root_hbm, root_v, 0)]}
    for d in (2, 1, 3, 0):
        for h in range(2):
            loads["w", d, h] = []
            for j in range(2):
                span = pl.ds(pl.multiple_of(chip(ring(a, d), 2 * h + j) * BLOCK, BLOCK), BLOCK)
                loads["w", d, h].append(fetch(w_hbm.at[span], w.at[span], 8 + 4 * d + 2 * h + j))
    offsets = [(i, j) for i in (2, 1, 3, 0) for j in (2, 1, 3, 0) if (i, j) != (0, 0)]
    partner = (2 * x + 1 - k, col)
    along = {
        "x": lambda d: (2 * ring(x, d) + k, col),
        "y": lambda d: (row, 4 * z + ring(y, d)),
        "z": lambda d: (row, 4 * ring(z, d) + y),
    }
    here = {"x": x, "y": y, "z": z}
    first_ring = (row, chip(ring(a, 1), b)), (row, chip(ring(a, 3), b))
    second_ring = lambda d: (row, chip(a, ring(b, d)))
    greet(
        [(row, plane(*o)) for o in offsets] + [along["x"](d) for d in (1, 2, 3)] + [partner]
    )
    links = Links(send, recv)
    def loaded(name):
        for copy in loads.pop(name, ()):
            copy.wait()

    loaded("root")
    root_t[...] = root_v[...].T
    passed = []

    def root_done():
        passed.append(1)
        if len(passed) == 1:
            loads["mid"] = [fetch(mid_hbm.at[x], mid_v, 1)]
            loads["c"] = [fetch(c_hbm, c, 2)]
            loads["dm"] = [fetch(dm_hbm, dm, 3)]
            loads["leaf"] = [fetch(leaf_hbm, leaf_v, 4)]
            loads["cl"] = [fetch(cl_hbm, cl, 5)]
        if len(passed) == groups:
            tall = w.shape[0]
            span = dl_hbm.shape[1]
            loads["dl"] = [
                fetch(
                    dl_hbm.at[i * tall : (i + 1) * tall], w.at[:, i * span : (i + 1) * span], 6 + i
                )
                for i in range(2)
            ]

    gathered, quarters, delivered = (ra_0, ra_1), (rq_0, rq_1), (t_0, t_1)

    def view(ra, base, part, third, done, axis, at, half):
        index = []
        lead = True
        split = half is not None
        for name in ("x", "k", "z", "y"):
            if name == "k":
                index.append(k)
            elif name == axis:
                index.append(at)
            elif name in done:
                if split and lead:
                    index.append(pl.ds(2 * half, 2))
                else:
                    index.append(slice(None))
                lead = False
            else:
                index.append(here[name])
        if split and not done:
            index.append(pl.ds(base + half * (third // 2), third // 2))
        else:
            index.append(pl.ds(base, third))
        return ra.at[tuple(index)]

    def program(g):
        lo = g * size
        ra, rq, t = gathered[g], quarters[g], delivered[g]
        rows = slice(lo, lo + size)
        tall = size // 2
        quarter = size // 4

        def root_term(d, h):
            loaded(("w", d, h))
            ids = [chip(ring(a, d), 2 * h + j) for j in range(2)]
            part = jnp.concatenate(
                [w[pl.ds(pl.multiple_of(i * BLOCK, BLOCK), BLOCK), :] for i in ids], axis=0
            )
            return lax.dot_general(root_t[rows, :], part, NT, preferred_element_type=F32)

        halves, used = yield from ring_sum(
            links, root_term, nothing, *first_ring,
            lambda i, h: sa.at[g, i, h, :, :wide], rf1r.at[g], rn1r.at[g],
            lambda i: pool.at[g, i, :, :wide],
        )
        root_done()
        for h in range(2):
            for j in range(2):
                y1[g, 2 * h + j, :, :BLOCK] = halves[h][:, j * BLOCK : (j + 1) * BLOCK]
        block, also = yield from ring_direct(
            links, lambda d: y1[g, ring(b, d), :, :BLOCK], second_ring,
            lambda i: sb.at[g, i, :, :BLOCK], rn2r.at[g],
        )
        used += also
        block = block.astype(BF)
        ra[x, k, z, y] = block
        out_root[rows, :] = block

        orders, third = ("xyz", "yzx", "zxy"), size // 3
        shared = []

        def share(ref):
            shared.append(links(ref, ref, partner))

        moved = []
        for part, order in enumerate(orders):
            own = ra.at[x, k, z, y, pl.ds(part * third, third)]
            moved += [links(own, own, along[order[0]](d)) for d in (2, 1, 3)]
        yield
        if "mid" in loads:
            loaded("mid")
            mid_t[...] = mid_v[...].T
            loaded("leaf")
            leaf_t[...] = leaf_v[...].T
        for copy in moved:
            copy.wait_recv()
        for phase in (1, 2):

            def piece(part, shift_by, half=None):
                order = orders[part]
                axis = order[phase]
                return view(
                    ra, part * third, part, third, order[:phase], axis, ring(here[axis], shift_by), half
                )

            state = []
            for part, order in enumerate(orders):
                own = piece(part, 0)
                axis = order[phase]
                state.append((links(own, own, along[axis](1)), links(own, own, along[axis](3))))
                if phase == 2:
                    share(own)
            yield
            onward = []
            for part, order in enumerate(orders):
                axis = order[phase]
                state[part][0].wait_recv()
                got = piece(part, 3, 0)
                first = links(got, got, along[axis](1))
                state[part][1].wait_recv()
                got = piece(part, 1, 1)
                onward.append((first, links(got, got, along[axis](3))))
                if phase == 2:
                    share(piece(part, 3))
                    share(piece(part, 1))
            yield
            for part in range(len(orders)):
                for half in range(2):
                    onward[part][half].wait_recv()
                    if phase == 2:
                        share(piece(part, 2, half))
        yield
        for copy in shared:
            copy.wait_recv()

        def root_block(v):
            return ra[
                lax.div(v, 32), lax.rem(lax.div(v, 16), 2), lax.rem(lax.div(v, 4), 4), lax.rem(v, 4)
            ]

        loaded("c")
        count = bm.shape[1] // 2
        for q in range(count // 16):
            for i in range(4):
                for j in range(4):
                    sp[g, i, :, j * BLOCK : (j + 1) * BLOCK] = root_block(
                        bm[x, k * count + q * 16 + i * 4 + j]
                    )
            left = jnp.concatenate([sp[g, i] for i in range(4)], axis=1)
            term = jnp.dot(
                left, c[q * 16 * BLOCK : (q + 1) * 16 * BLOCK, :], preferred_element_type=F32
            )
            if q == 0:
                pool[g, 0] = term
            else:
                pool[g, 0] += term
        swap = links(pool.at[g, 0], exr.at[g], partner)
        yield
        swap.wait_recv()
        shift[g] = (mid_t[rows, :].astype(F32) - (pool[g, 0] + exr[g])).astype(BF)
        links.sent(used + [swap])
        loaded("dm")

        def mid_term(d, h):
            ids = [chip(ring(a, d), 2 * h + j) for j in range(2)]
            part = jnp.concatenate(
                [dm[pl.ds(pl.multiple_of(i * wide, wide), wide), :] for i in ids], axis=0
            )
            return lax.dot_general(shift[g], part, NT, preferred_element_type=F32)

        halves, used = yield from ring_sum(
            links, mid_term, nothing, *first_ring,
            lambda i, h: sa.at[g, i, h], rf1m.at[g], rn1m.at[g], lambda i: pool.at[g, i],
        )
        for h in range(2):
            for j in range(2):
                y1[g, 2 * h + j] = halves[h][:, j * wide : (j + 1) * wide]
        block, also = yield from ring_direct(
            links, lambda d: y1[g, ring(b, d)], second_ring, lambda i: sb.at[g, i], rn2m.at[g]
        )
        used += also
        block = block.astype(BF)
        out_mid[rows, :] = block
        for i in range(4):
            for j in range(2):
                m4[g, i, j] = block[i * quarter : (i + 1) * quarter, j * BLOCK : (j + 1) * BLOCK]

        moved = []
        for d in (2, 1, 3):
            q = ring(x, d)
            moved.append(links(m4.at[g, q], rq.at[x], (2 * q + k, col)))
        rq[x] = m4[g, x]
        yield
        for copy in moved:
            copy.wait_recv()
        moved = []
        for i, (dz, dy) in enumerate(offsets):
            to = plane(dz, dy)
            ts[g, i] = rq[parents[to]]
            moved.append(links(ts.at[g, i], t.at[k, col], (row, to)))
        t[k, col] = rq[parents[col]]
        shared = [links(t.at[k, col], t.at[k, col], partner)]
        yield
        for i, (copy, (dz, dy)) in enumerate(zip(moved, offsets)):
            copy.wait_recv()
            got = t.at[k, plane(4 - dz, 4 - dy)]
            shared.append(links(got, got, partner))
            if i % 5 == 4:
                yield
        for copy in shared:
            copy.wait_recv()
        slots = u.shape[2]

        def parent_block(v):
            m = jnp.maximum(v - 128, 0)
            return t[lax.div(m, 32), lax.div(lax.rem(m, 32), 2), lax.rem(m, 2)]

        moved = []
        for d in (2, 1, 3):
            q = ring(x, d)
            for i in range(slots):
                u[g, d - 1, i] = parent_block(bl[col, (2 * q + k) * slots + i])
            moved.append(links(u.at[g, d - 1], bb.at[g, x], (2 * q + k, col)))
        for i in range(slots):
            bb[g, x, i] = parent_block(bl[col, row * slots + i])
        links.sent(used)
        yield
        for copy in moved:
            copy.wait_recv()
        for i in range(slots):
            v = bl[col, row * slots + i]
            side = root_block(jnp.minimum(v, 127)).astype(F32)
            for q in range(4):
                span = slice(q * quarter, (q + 1) * quarter)
                bound[g, span, i * BLOCK : (i + 1) * BLOCK] = jnp.where(
                    v < 128, side[span, :], bb[g, q, i].astype(F32)
                ).astype(BF)

        up, down = along["x"](1), along["x"](3)
        length = shift.shape[2]

        def scatter(product, rp, base, rf, rn):
            out = {}

            def make(d):
                q = ring(x, d)
                sp[g, d] = product(q, 1 - k).astype(BF)
                out[d] = links(sp.at[g, d], rp.at[g, d], partner)
                pool[g, d] = product(q, k)

            def prepare(d):
                if d == 2:
                    make(2)
                    make(1)
                    yield
                elif d == 1:
                    make(3)
                    yield
                elif d == 3:
                    make(0)
                out[d].wait_recv()

            def value(d, h):
                span = slice(h * tall, (h + 1) * tall)
                return pool[g, d, span, :] + rp[g, d, span, :].astype(F32)

            halves, used = yield from ring_sum(
                links, value, prepare, up, down,
                lambda i, h: sa.at[g, i, h, base : base + tall], rf.at[g], rn.at[g], None,
            )
            return halves, list(out.values())

        loaded("cl")
        halves, used = yield from scatter(
            lambda q, core: jnp.dot(
                bound[g],
                cl[:, pl.ds(pl.multiple_of((2 * q + core) * length, length), length)],
                preferred_element_type=F32,
            ),
            rp1, 0, rf1l, rn1l,
        )
        for h in range(2):
            shift[g, h * tall : (h + 1) * tall, :] = (
                leaf_t[lo + h * tall : lo + (h + 1) * tall, :].astype(F32) - halves[h]
            ).astype(BF)
        links.sent(used)
        loaded("dl")
        halves, used = yield from scatter(
            lambda q, core: lax.dot_general(
                shift[g],
                w[
                    pl.ds(pl.multiple_of((2 * lax.rem(q, 2) + core) * length, length), length),
                    pl.ds(pl.multiple_of(lax.div(q, 2) * length, length), length),
                ],
                NT,
                preferred_element_type=F32,
            ),
            rp2, tall, rf2l, rn2l,
        )
        for h in range(2):
            out_leaf[lo + h * tall : lo + (h + 1) * tall, :] = halves[h].astype(BF)

    together([program(g) for g in range(groups)], lag)
    links.drain()
    assert len(links.made) == send.shape[0], len(links.made)


def turned(*refs):
    half = len(refs) // 2
    for source, target in zip(refs[:half], refs[half:]):
        target[...] = source[...].T


VM = pl.BlockSpec(memory_space=pltpu.VMEM)
SM = pl.BlockSpec(memory_space=pltpu.SMEM)
ANY = pl.BlockSpec(memory_space=pl.ANY)
GROUPS = 2
COPIES = 124
LAG = 0


def shards(
    dinv_root, rhs_root, dinv_mid, coup_mid, rhs_mid, dinv_leaf, coup_leaf, rhs_leaf,
    bounds_mid, bounds_leaf, parents,
):
    n = rhs_root.shape[1]
    slots = bounds_leaf.shape[1] // 8
    wide = 2 * BLOCK
    length = rhs_leaf.shape[1]
    g, r = GROUPS, n // GROUPS
    scratch = [
        (rhs_root.shape, BF), (rhs_root.shape[::-1], BF),
        (rhs_mid.shape[1:], BF), ((n, length), BF), (rhs_leaf.shape[1:], BF), ((n, length), BF),
        (dinv_root.shape, BF), (coup_mid.shape, BF), (dinv_mid.shape, BF), (coup_leaf.shape[1:], BF),
        ((4, 2, 4, 4, r, BLOCK), BF), ((4, 2, 4, 4, r, BLOCK), BF),
        ((g, 4, r, length), F32), ((g, 4, r, wide), F32),
        ((g, 3, 2, r, length), BF), ((g, 3, r, wide), BF),
        ((g, 2, r, wide), BF), ((g, 2, 2, r, wide), BF),
        ((g, 3, r, BLOCK), BF),
        ((g, 2, r, length), BF), ((g, 2, 2, r, length), BF),
        ((g, 3, r, wide), BF),
        ((g, r, length), F32), ((g, r, length), BF),
        ((g, 4, 2, r // 4, BLOCK), BF), ((4, 2, r // 4, BLOCK), BF), ((4, 2, r // 4, BLOCK), BF),
        ((g, 15, 2, r // 4, BLOCK), BF), ((2, 16, 2, r // 4, BLOCK), BF), ((2, 16, 2, r // 4, BLOCK), BF),
        ((g, 3, slots, r // 4, BLOCK), BF), ((g, 4, slots, r // 4, BLOCK), BF),
        ((g, r, slots * BLOCK), BF),
        ((g, 4, r, length), BF), ((g, 4, r, length), BF), ((g, 4, r, length), BF),
        ((g, 2, r // 2, length), BF), ((g, 2, 2, r // 2, length), BF),
        ((g, 2, r // 2, length), BF), ((g, 2, 2, r // 2, length), BF),
    ]
    copies = COPIES * g
    outs = pl.pallas_call(
        functools.partial(kernel, GROUPS, LAG),
        out_shape=tuple(jax.ShapeDtypeStruct((n, width), BF) for width in (BLOCK, wide, length)),
        in_specs=[SM] * 3 + [ANY] * 8,
        out_specs=(VM,) * 3,
        scratch_shapes=[pltpu.VMEM(shape, kind) for shape, kind in scratch]
        + [
            pltpu.SemaphoreType.DMA((24,)),
            pltpu.SemaphoreType.DMA((copies,)),
            pltpu.SemaphoreType.DMA((copies,)),
        ],
        compiler_params=pltpu.CompilerParams(
            collective_id=0, has_side_effects=True, vmem_limit_bytes=67043328
        ),
    )(
        bounds_mid, bounds_leaf, parents, rhs_root, rhs_mid, rhs_leaf[0],
        dinv_root, coup_mid, dinv_mid, coup_leaf[0], dinv_leaf[0],
    )
    root, mid, leaf = pl.pallas_call(
        turned,
        out_shape=tuple(jax.ShapeDtypeStruct(out.shape[::-1], BF) for out in outs),
        in_specs=[VM] * 3,
        out_specs=(VM,) * 3,
    )(*outs)
    return root, mid, leaf[None]


def solution(mesh):
    return jax.shard_map(
        shards,
        mesh=mesh,
        in_specs=(
            P("row", "col"),
            P("col", None),
            P("row", "col"),
            P("row", "col"),
            P(None, "col", None),
            P("col", None, "row"),
            P("col", "row", None),
            P("col", "row", None),
            P(),
            P(),
            P(),
        ),
        out_specs=(P(("row", "col"), None), P(("row", "col"), None), P("col", "row", None)),
        check_vma=False,
    )
```

```python
import functools

import jax
import jax.numpy as jnp
from jax import lax
from jax.experimental import pallas as pl
from jax.experimental.pallas import tpu as pltpu
from jax.sharding import PartitionSpec as P

MESH = pl.DeviceIdType.MESH
BF = jnp.bfloat16
F32 = jnp.float32
BLOCK = 128
NT = (((1,), (1,)), ((), ()))


def position():
    row, col = lax.axis_index("row"), lax.axis_index("col")
    return row, col, lax.div(row, 2), lax.rem(row, 2), lax.div(col, 4), lax.rem(col, 4)


def ring(p, d):
    return lax.rem(p + d, 4)


class Links:
    def __init__(self, send, recv):
        self.send, self.recv, self.made, self.done = send, recv, [], set()

    def __call__(self, src, dst, device):
        i = len(self.made)
        copy = pltpu.make_async_remote_copy(
            src_ref=src,
            dst_ref=dst,
            send_sem=self.send.at[i],
            recv_sem=self.recv.at[i],
            device_id=device,
            device_id_type=MESH,
        )
        copy.start()
        self.made.append(copy)
        return copy

    def sent(self, copies):
        for copy in copies:
            if id(copy) not in self.done:
                self.done.add(id(copy))
                copy.wait_send()

    def drain(self):
        self.sent(self.made)


def greet(peers, meanwhile):
    barrier = pltpu.get_barrier_semaphore()
    for peer in peers:
        pl.semaphore_signal(barrier, inc=1, device_id=peer, device_id_type=MESH)
    meanwhile()
    pl.semaphore_wait(barrier, len(peers))


def ring_sum(links, value, prepare, up, down, s, rf, rn, p):
    prepare(2)
    s(1, 0)[...] = value(2, 0).astype(BF)
    far_up = links(s(1, 0), rf.at[0], up)
    s(1, 1)[...] = value(2, 1).astype(BF)
    far_down = links(s(1, 1), rf.at[1], down)
    yield
    prepare(1)
    s(0, 1)[...] = value(1, 1).astype(BF)
    last = [links(s(0, 1), rn.at[0, 1], up)]
    prepare(3)
    s(2, 0)[...] = value(3, 0).astype(BF)
    last.append(links(s(2, 0), rn.at[1, 0], down))
    if p is not None:
        for i, term in enumerate(((1, 0), (3, 1), (0, 0), (0, 1))):
            p(i)[...] = value(*term)
    kept = (lambda i, d, h: p(i)[...]) if p is not None else (lambda i, d, h: value(d, h))
    yield
    far_up.wait_recv()
    s(0, 0)[...] = (kept(0, 1, 0) + rf[0].astype(F32)).astype(BF)
    last.append(links(s(0, 0), rn.at[0, 0], up))
    yield
    far_down.wait_recv()
    s(2, 1)[...] = (kept(1, 3, 1) + rf[1].astype(F32)).astype(BF)
    last.append(links(s(2, 1), rn.at[1, 1], down))
    prepare(0)
    yield
    for copy in last:
        copy.wait_recv()
    halves = [
        kept(2 + h, 0, h) + rn[0, h].astype(F32) + rn[1, h].astype(F32) for h in range(2)
    ]
    return halves, last + [far_up, far_down]


def ring_direct(links, value, to, s, rn):
    moved = []
    for d in (2, 1, 3):
        s(d - 1)[...] = value(d).astype(BF)
        moved.append(links(s(d - 1), rn.at[d - 1], to(d)))
    yield
    total = value(0)
    for copy, d in zip(moved, (2, 1, 3)):
        copy.wait_recv()
        total += rn[d - 1].astype(F32)
    return total, moved


def nothing(d):
    pass


def together(programs, lag):
    turn, live = 0, list(enumerate(programs))
    while live:
        for item in list(live):
            if turn >= item[0] * lag:
                try:
                    next(item[1])
                except StopIteration:
                    live.remove(item)
        turn += 1


def kernel(
    groups, lag,
    bm, bl, parents, root_hbm, mid_hbm, leaf_hbm, w_hbm, c_hbm, dm_hbm, cl_hbm, dl_hbm,
    out_root, out_mid, out_leaf,
    root_v, root_t, mid_v, mid_t, leaf_v, leaf_t,
    w, c, dm, cl, ra_0, ra_1, pool, y1, sa, sb,
    rf1r, rn1r, rn2r, rf1m, rn1m, rn2m, exr, shift,
    m4, rq_0, rq_1, ts, t_0, t_1, u, bb, bound, sp, rp1, rp2, rf1l, rn1l, rf2l, rn2l,
    local, send, recv,
):
    row, col, x, k, z, y = position()
    a, b = k * z + (1 - k) * y, k * y + (1 - k) * z
    size = root_t.shape[0] // groups
    wide = 2 * BLOCK

    def chip(a_, b_):
        return k * (4 * a_ + b_) + (1 - k) * (4 * b_ + a_)

    def plane(dz, dy):
        return 4 * ring(z, dz) + ring(y, dy)

    def fetch(source, target, i):
        copy = pltpu.make_async_copy(source, target, local.at[i])
        copy.start()
        return copy

    loads = {"root": [fetch(root_hbm, root_v, 0)]}
    for d in (2, 1, 3, 0):
        for h in range(2):
            loads["w", d, h] = []
            for j in range(2):
                span = pl.ds(pl.multiple_of(chip(ring(a, d), 2 * h + j) * BLOCK, BLOCK), BLOCK)
                loads["w", d, h].append(fetch(w_hbm.at[span], w.at[span], 8 + 4 * d + 2 * h + j))
    offsets = [(i, j) for i in (2, 1, 3, 0) for j in (2, 1, 3, 0) if (i, j) != (0, 0)]
    partner = (2 * x + 1 - k, col)
    along = {
        "x": lambda d: (2 * ring(x, d) + k, col),
        "y": lambda d: (row, 4 * z + ring(y, d)),
        "z": lambda d: (row, 4 * ring(z, d) + y),
    }
    here = {"x": x, "y": y, "z": z}
    first_ring = (row, chip(ring(a, 1), b)), (row, chip(ring(a, 3), b))
    second_ring = lambda d: (row, chip(a, ring(b, d)))
    def loaded(name):
        for copy in loads.pop(name, ()):
            copy.wait()

    def turn_root():
        loaded("root")
        root_t[...] = root_v[...].T

    greet(
        [(row, plane(*o)) for o in offsets] + [along["x"](d) for d in (1, 2, 3)] + [partner],
        turn_root,
    )
    links = Links(send, recv)
    passed = []

    def root_done():
        passed.append(1)
        if len(passed) == 1:
            loads["mid"] = [fetch(mid_hbm.at[x], mid_v, 1)]
            loads["c"] = [fetch(c_hbm, c, 2)]
            loads["dm"] = [fetch(dm_hbm, dm, 3)]
            loads["leaf"] = [fetch(leaf_hbm, leaf_v, 4)]
            loads["cl"] = [fetch(cl_hbm, cl, 5)]
        if len(passed) == groups:
            tall = w.shape[0]
            span = dl_hbm.shape[1]
            loads["dl"] = [
                fetch(
                    dl_hbm.at[i * tall : (i + 1) * tall], w.at[:, i * span : (i + 1) * span], 6 + i
                )
                for i in range(2)
            ]

    gathered, quarters, delivered = (ra_0, ra_1), (rq_0, rq_1), (t_0, t_1)

    def view(ra, base, part, third, done, axis, at, half):
        index = []
        lead = True
        split = half is not None
        for name in ("x", "k", "z", "y"):
            if name == "k":
                index.append(k)
            elif name == axis:
                index.append(at)
            elif name in done:
                if split and lead:
                    index.append(pl.ds(2 * half, 2))
                else:
                    index.append(slice(None))
                lead = False
            else:
                index.append(here[name])
        if split and not done:
            index.append(pl.ds(base + half * (third // 2), third // 2))
        else:
            index.append(pl.ds(base, third))
        return ra.at[tuple(index)]

    def program(g):
        lo = g * size
        ra, rq, t = gathered[g], quarters[g], delivered[g]
        rows = slice(lo, lo + size)
        tall = size // 2
        quarter = size // 4

        def root_term(d, h):
            loaded(("w", d, h))
            ids = [chip(ring(a, d), 2 * h + j) for j in range(2)]
            part = jnp.concatenate(
                [w[pl.ds(pl.multiple_of(i * BLOCK, BLOCK), BLOCK), :] for i in ids], axis=0
            )
            return lax.dot_general(root_t[rows, :], part, NT, preferred_element_type=F32)

        halves, used = yield from ring_sum(
            links, root_term, nothing, *first_ring,
            lambda i, h: sa.at[g, i, h, :, :wide], rf1r.at[g], rn1r.at[g],
            lambda i: pool.at[g, i, :, :wide],
        )
        root_done()
        for h in range(2):
            for j in range(2):
                y1[g, 2 * h + j, :, :BLOCK] = halves[h][:, j * BLOCK : (j + 1) * BLOCK]
        block, also = yield from ring_direct(
            links, lambda d: y1[g, ring(b, d), :, :BLOCK], second_ring,
            lambda i: sb.at[g, i, :, :BLOCK], rn2r.at[g],
        )
        used += also
        block = block.astype(BF)
        ra[x, k, z, y] = block
        out_root[rows, :] = block

        orders, third = ("xyz", "yzx", "zxy"), size // 3
        shared = []

        def share(ref):
            shared.append(links(ref, ref, partner))

        moved = []
        for part, order in enumerate(orders):
            own = ra.at[x, k, z, y, pl.ds(part * third, third)]
            moved += [links(own, own, along[order[0]](d)) for d in (2, 1, 3)]
        yield
        if "mid" in loads:
            loaded("mid")
            mid_t[...] = mid_v[...].T
            loaded("leaf")
            leaf_t[...] = leaf_v[...].T
        for copy in moved:
            copy.wait_recv()
        for phase in (1, 2):

            def piece(part, shift_by, half=None):
                order = orders[part]
                axis = order[phase]
                return view(
                    ra, part * third, part, third, order[:phase], axis, ring(here[axis], shift_by), half
                )

            state = []
            for part, order in enumerate(orders):
                own = piece(part, 0)
                axis = order[phase]
                state.append((links(own, own, along[axis](1)), links(own, own, along[axis](3))))
                if phase == 2:
                    share(own)
            yield
            onward = []
            for part, order in enumerate(orders):
                axis = order[phase]
                state[part][0].wait_recv()
                got = piece(part, 3, 0)
                first = links(got, got, along[axis](1))
                state[part][1].wait_recv()
                got = piece(part, 1, 1)
                onward.append((first, links(got, got, along[axis](3))))
                if phase == 2:
                    share(piece(part, 3))
                    share(piece(part, 1))
            yield
            for part in range(len(orders)):
                for half in range(2):
                    onward[part][half].wait_recv()
                    if phase == 2:
                        share(piece(part, 2, half))
        yield
        for copy in shared:
            copy.wait_recv()

        def root_block(v):
            return ra[
                lax.div(v, 32), lax.rem(lax.div(v, 16), 2), lax.rem(lax.div(v, 4), 4), lax.rem(v, 4)
            ]

        loaded("c")
        count = bm.shape[1] // 2
        for q in range(count // 16):
            for i in range(4):
                for j in range(4):
                    sp[g, i, :, j * BLOCK : (j + 1) * BLOCK] = root_block(
                        bm[x, k * count + q * 16 + i * 4 + j]
                    )
            left = jnp.concatenate([sp[g, i] for i in range(4)], axis=1)
            term = jnp.dot(
                left, c[q * 16 * BLOCK : (q + 1) * 16 * BLOCK, :], preferred_element_type=F32
            )
            if q == 0:
                pool[g, 0] = term
            else:
                pool[g, 0] += term
        swap = links(pool.at[g, 0], exr.at[g], partner)
        yield
        swap.wait_recv()
        shift[g] = (mid_t[rows, :].astype(F32) - (pool[g, 0] + exr[g])).astype(BF)
        links.sent(used + [swap])
        loaded("dm")

        def mid_term(d, h):
            ids = [chip(ring(a, d), 2 * h + j) for j in range(2)]
            part = jnp.concatenate(
                [dm[pl.ds(pl.multiple_of(i * wide, wide), wide), :] for i in ids], axis=0
            )
            return lax.dot_general(shift[g], part, NT, preferred_element_type=F32)

        halves, used = yield from ring_sum(
            links, mid_term, nothing, *first_ring,
            lambda i, h: sa.at[g, i, h], rf1m.at[g], rn1m.at[g], lambda i: pool.at[g, i],
        )
        for h in range(2):
            for j in range(2):
                y1[g, 2 * h + j] = halves[h][:, j * wide : (j + 1) * wide]
        block, also = yield from ring_direct(
            links, lambda d: y1[g, ring(b, d)], second_ring, lambda i: sb.at[g, i], rn2m.at[g]
        )
        used += also
        block = block.astype(BF)
        out_mid[rows, :] = block
        for i in range(4):
            for j in range(2):
                m4[g, i, j] = block[i * quarter : (i + 1) * quarter, j * BLOCK : (j + 1) * BLOCK]

        moved = []
        for d in (2, 1, 3):
            q = ring(x, d)
            moved.append(links(m4.at[g, q], rq.at[x], (2 * q + k, col)))
        rq[x] = m4[g, x]
        yield
        for copy in moved:
            copy.wait_recv()
        moved = []
        for i, (dz, dy) in enumerate(offsets):
            to = plane(dz, dy)
            ts[g, i] = rq[parents[to]]
            moved.append(links(ts.at[g, i], t.at[k, col], (row, to)))
        t[k, col] = rq[parents[col]]
        shared = [links(t.at[k, col], t.at[k, col], partner)]
        yield
        for copy, (dz, dy) in zip(moved, offsets):
            copy.wait_recv()
            got = t.at[k, plane(4 - dz, 4 - dy)]
            shared.append(links(got, got, partner))
        for copy in shared:
            copy.wait_recv()
        slots = u.shape[2]

        def parent_block(v):
            m = jnp.maximum(v - 128, 0)
            return t[lax.div(m, 32), lax.div(lax.rem(m, 32), 2), lax.rem(m, 2)]

        moved = []
        for d in (2, 1, 3):
            q = ring(x, d)
            for i in range(slots):
                u[g, d - 1, i] = parent_block(bl[col, (2 * q + k) * slots + i])
            moved.append(links(u.at[g, d - 1], bb.at[g, x], (2 * q + k, col)))
        for i in range(slots):
            bb[g, x, i] = parent_block(bl[col, row * slots + i])
        links.sent(used)
        yield
        for copy in moved:
            copy.wait_recv()
        for i in range(slots):
            v = bl[col, row * slots + i]
            side = root_block(jnp.minimum(v, 127)).astype(F32)
            for q in range(4):
                span = slice(q * quarter, (q + 1) * quarter)
                bound[g, span, i * BLOCK : (i + 1) * BLOCK] = jnp.where(
                    v < 128, side[span, :], bb[g, q, i].astype(F32)
                ).astype(BF)

        up, down = along["x"](1), along["x"](3)
        length = shift.shape[2]

        def scatter(product, rp, base, rf, rn):
            out = {}

            def make(d):
                q = ring(x, d)
                sp[g, d] = product(q, 1 - k).astype(BF)
                out[d] = links(sp.at[g, d], rp.at[g, d], partner)
                pool[g, d] = product(q, k)

            def prepare(d):
                if d == 2:
                    make(2)
                    make(1)
                elif d == 1:
                    make(3)
                elif d == 3:
                    make(0)
                out[d].wait_recv()

            def value(d, h):
                span = slice(h * tall, (h + 1) * tall)
                return pool[g, d, span, :] + rp[g, d, span, :].astype(F32)

            halves, used = yield from ring_sum(
                links, value, prepare, up, down,
                lambda i, h: sa.at[g, i, h, base : base + tall], rf.at[g], rn.at[g], None,
            )
            return halves, list(out.values())

        loaded("cl")
        halves, used = yield from scatter(
            lambda q, core: jnp.dot(
                bound[g],
                cl[:, pl.ds(pl.multiple_of((2 * q + core) * length, length), length)],
                preferred_element_type=F32,
            ),
            rp1, 0, rf1l, rn1l,
        )
        for h in range(2):
            shift[g, h * tall : (h + 1) * tall, :] = (
                leaf_t[lo + h * tall : lo + (h + 1) * tall, :].astype(F32) - halves[h]
            ).astype(BF)
        links.sent(used)
        loaded("dl")
        halves, used = yield from scatter(
            lambda q, core: lax.dot_general(
                shift[g],
                w[
                    pl.ds(pl.multiple_of((2 * lax.rem(q, 2) + core) * length, length), length),
                    pl.ds(pl.multiple_of(lax.div(q, 2) * length, length), length),
                ],
                NT,
                preferred_element_type=F32,
            ),
            rp2, tall, rf2l, rn2l,
        )
        for h in range(2):
            out_leaf[lo + h * tall : lo + (h + 1) * tall, :] = halves[h].astype(BF)

    together([program(g) for g in range(groups)], lag)
    links.drain()
    assert len(links.made) == send.shape[0], len(links.made)


def turned(*refs):
    half = len(refs) // 2
    for source, target in zip(refs[:half], refs[half:]):
        target[...] = source[...].T


VM = pl.BlockSpec(memory_space=pltpu.VMEM)
SM = pl.BlockSpec(memory_space=pltpu.SMEM)
ANY = pl.BlockSpec(memory_space=pl.ANY)
GROUPS = 2
COPIES = 124
LAG = 0


def shards(
    dinv_root, rhs_root, dinv_mid, coup_mid, rhs_mid, dinv_leaf, coup_leaf, rhs_leaf,
    bounds_mid, bounds_leaf, parents,
):
    n = rhs_root.shape[1]
    slots = bounds_leaf.shape[1] // 8
    wide = 2 * BLOCK
    length = rhs_leaf.shape[1]
    g, r = GROUPS, n // GROUPS
    scratch = [
        (rhs_root.shape, BF), (rhs_root.shape[::-1], BF),
        (rhs_mid.shape[1:], BF), ((n, length), BF), (rhs_leaf.shape[1:], BF), ((n, length), BF),
        (dinv_root.shape, BF), (coup_mid.shape, BF), (dinv_mid.shape, BF), (coup_leaf.shape[1:], BF),
        ((4, 2, 4, 4, r, BLOCK), BF), ((4, 2, 4, 4, r, BLOCK), BF),
        ((g, 4, r, length), F32), ((g, 4, r, wide), F32),
        ((g, 3, 2, r, length), BF), ((g, 3, r, wide), BF),
        ((g, 2, r, wide), BF), ((g, 2, 2, r, wide), BF),
        ((g, 3, r, BLOCK), BF),
        ((g, 2, r, length), BF), ((g, 2, 2, r, length), BF),
        ((g, 3, r, wide), BF),
        ((g, r, length), F32), ((g, r, length), BF),
        ((g, 4, 2, r // 4, BLOCK), BF), ((4, 2, r // 4, BLOCK), BF), ((4, 2, r // 4, BLOCK), BF),
        ((g, 15, 2, r // 4, BLOCK), BF), ((2, 16, 2, r // 4, BLOCK), BF), ((2, 16, 2, r // 4, BLOCK), BF),
        ((g, 3, slots, r // 4, BLOCK), BF), ((g, 4, slots, r // 4, BLOCK), BF),
        ((g, r, slots * BLOCK), BF),
        ((g, 4, r, length), BF), ((g, 4, r, length), BF), ((g, 4, r, length), BF),
        ((g, 2, r // 2, length), BF), ((g, 2, 2, r // 2, length), BF),
        ((g, 2, r // 2, length), BF), ((g, 2, 2, r // 2, length), BF),
    ]
    copies = COPIES * g
    outs = pl.pallas_call(
        functools.partial(kernel, GROUPS, LAG),
        out_shape=tuple(jax.ShapeDtypeStruct((n, width), BF) for width in (BLOCK, wide, length)),
        in_specs=[SM] * 3 + [ANY] * 8,
        out_specs=(VM,) * 3,
        scratch_shapes=[pltpu.VMEM(shape, kind) for shape, kind in scratch]
        + [
            pltpu.SemaphoreType.DMA((24,)),
            pltpu.SemaphoreType.DMA((copies,)),
            pltpu.SemaphoreType.DMA((copies,)),
        ],
        compiler_params=pltpu.CompilerParams(
            collective_id=0, has_side_effects=True, vmem_limit_bytes=67043328
        ),
    )(
        bounds_mid, bounds_leaf, parents, rhs_root, rhs_mid, rhs_leaf[0],
        dinv_root, coup_mid, dinv_mid, coup_leaf[0], dinv_leaf[0],
    )
    root, mid, leaf = pl.pallas_call(
        turned,
        out_shape=tuple(jax.ShapeDtypeStruct(out.shape[::-1], BF) for out in outs),
        in_specs=[VM] * 3,
        out_specs=(VM,) * 3,
    )(*outs)
    return root, mid, leaf[None]


def solution(mesh):
    return jax.shard_map(
        shards,
        mesh=mesh,
        in_specs=(
            P("row", "col"),
            P("col", None),
            P("row", "col"),
            P("row", "col"),
            P(None, "col", None),
            P("col", None, "row"),
            P("col", "row", None),
            P("col", "row", None),
            P(),
            P(),
            P(),
        ),
        out_specs=(P(("row", "col"), None), P(("row", "col"), None), P("col", "row", None)),
        check_vma=False,
    )
```

```python
import functools

import jax
import jax.numpy as jnp
from jax import lax
from jax.experimental import pallas as pl
from jax.experimental.pallas import tpu as pltpu
from jax.sharding import PartitionSpec as P

MESH = pl.DeviceIdType.MESH
BF = jnp.bfloat16
F32 = jnp.float32
BLOCK = 128
NT = (((1,), (1,)), ((), ()))


def position():
    row, col = lax.axis_index("row"), lax.axis_index("col")
    return row, col, lax.div(row, 2), lax.rem(row, 2), lax.div(col, 4), lax.rem(col, 4)


def ring(p, d):
    return lax.rem(p + d, 4)


class Links:
    def __init__(self, send, recv):
        self.send, self.recv, self.made, self.done = send, recv, [], set()

    def __call__(self, src, dst, device):
        i = len(self.made)
        copy = pltpu.make_async_remote_copy(
            src_ref=src,
            dst_ref=dst,
            send_sem=self.send.at[i],
            recv_sem=self.recv.at[i],
            device_id=device,
            device_id_type=MESH,
        )
        copy.start()
        self.made.append(copy)
        return copy

    def sent(self, copies):
        for copy in copies:
            if id(copy) not in self.done:
                self.done.add(id(copy))
                copy.wait_send()

    def drain(self):
        self.sent(self.made)


def greet(peers, meanwhile):
    barrier = pltpu.get_barrier_semaphore()
    for peer in peers:
        pl.semaphore_signal(barrier, inc=1, device_id=peer, device_id_type=MESH)
    meanwhile()
    pl.semaphore_wait(barrier, len(peers))


def ring_sum(links, value, prepare, up, down, s, rf, rn, p):
    prepare(2)
    s(1, 0)[...] = value(2, 0).astype(BF)
    far_up = links(s(1, 0), rf.at[0], up)
    s(1, 1)[...] = value(2, 1).astype(BF)
    far_down = links(s(1, 1), rf.at[1], down)
    yield
    prepare(1)
    s(0, 1)[...] = value(1, 1).astype(BF)
    last = [links(s(0, 1), rn.at[0, 1], up)]
    prepare(3)
    s(2, 0)[...] = value(3, 0).astype(BF)
    last.append(links(s(2, 0), rn.at[1, 0], down))
    if p is not None:
        for i, term in enumerate(((1, 0), (3, 1))):
            p(i)[...] = value(*term)
    kept = (lambda i, d, h: p(i)[...]) if p is not None else (lambda i, d, h: value(d, h))
    yield
    far_up.wait_recv()
    s(0, 0)[...] = (kept(0, 1, 0) + rf[0].astype(F32)).astype(BF)
    last.append(links(s(0, 0), rn.at[0, 0], up))
    far_down.wait_recv()
    s(2, 1)[...] = (kept(1, 3, 1) + rf[1].astype(F32)).astype(BF)
    last.append(links(s(2, 1), rn.at[1, 1], down))
    prepare(0)
    if p is not None:
        for i, term in enumerate(((0, 0), (0, 1))):
            p(2 + i)[...] = value(*term)
    yield
    for copy in last:
        copy.wait_recv()
    halves = [
        kept(2 + h, 0, h) + rn[0, h].astype(F32) + rn[1, h].astype(F32) for h in range(2)
    ]
    return halves, last + [far_up, far_down]


def ring_direct(links, value, to, s, rn):
    moved = []
    for d in (2, 1, 3):
        s(d - 1)[...] = value(d).astype(BF)
        moved.append(links(s(d - 1), rn.at[d - 1], to(d)))
    yield
    total = value(0)
    for copy, d in zip(moved, (2, 1, 3)):
        copy.wait_recv()
        total += rn[d - 1].astype(F32)
    return total, moved


def nothing(d):
    pass


def together(programs, lag):
    turn, live = 0, list(enumerate(programs))
    while live:
        for item in list(live):
            if turn >= item[0] * lag:
                try:
                    next(item[1])
                except StopIteration:
                    live.remove(item)
        turn += 1


def kernel(
    groups, lag,
    bm, bl, parents, root_hbm, mid_hbm, leaf_hbm, w_hbm, c_hbm, dm_hbm, cl_hbm, dl_hbm,
    out_root, out_mid, out_leaf,
    root_v, root_t, mid_v, mid_t, leaf_v, leaf_t,
    w, c, dm, cl, ra_0, ra_1, pool, y1, sa, sb,
    rf1r, rn1r, rn2r, rf1m, rn1m, rn2m, exr, shift,
    m4, rq_0, rq_1, ts, t_0, t_1, u, bb, bound, sp, rp1, rp2, rf1l, rn1l, rf2l, rn2l,
    local, send, recv,
):
    row, col, x, k, z, y = position()
    a, b = k * z + (1 - k) * y, k * y + (1 - k) * z
    size = root_t.shape[0] // groups
    wide = 2 * BLOCK

    def chip(a_, b_):
        return k * (4 * a_ + b_) + (1 - k) * (4 * b_ + a_)

    def plane(dz, dy):
        return 4 * ring(z, dz) + ring(y, dy)

    def fetch(source, target, i):
        copy = pltpu.make_async_copy(source, target, local.at[i])
        copy.start()
        return copy

    loads = {"root": [fetch(root_hbm, root_v, 0)]}
    for d in (2, 1, 3, 0):
        for h in range(2):
            loads["w", d, h] = []
            for j in range(2):
                span = pl.ds(pl.multiple_of(chip(ring(a, d), 2 * h + j) * BLOCK, BLOCK), BLOCK)
                loads["w", d, h].append(fetch(w_hbm.at[span], w.at[span], 8 + 4 * d + 2 * h + j))
    offsets = [(i, j) for i in (2, 1, 3, 0) for j in (2, 1, 3, 0) if (i, j) != (0, 0)]
    partner = (2 * x + 1 - k, col)
    along = {
        "x": lambda d: (2 * ring(x, d) + k, col),
        "y": lambda d: (row, 4 * z + ring(y, d)),
        "z": lambda d: (row, 4 * ring(z, d) + y),
    }
    here = {"x": x, "y": y, "z": z}
    first_ring = (row, chip(ring(a, 1), b)), (row, chip(ring(a, 3), b))
    second_ring = lambda d: (row, chip(a, ring(b, d)))
    def loaded(name):
        for copy in loads.pop(name, ()):
            copy.wait()

    def turn_root():
        loaded("root")
        root_t[...] = root_v[...].T

    greet(
        [(row, plane(*o)) for o in offsets] + [along["x"](d) for d in (1, 2, 3)] + [partner],
        turn_root,
    )
    links = Links(send, recv)
    passed = []

    def root_done():
        passed.append(1)
        if len(passed) == 1:
            loads["mid"] = [fetch(mid_hbm.at[x], mid_v, 1)]
            loads["c"] = [fetch(c_hbm, c, 2)]
            loads["dm"] = [fetch(dm_hbm, dm, 3)]
            loads["leaf"] = [fetch(leaf_hbm, leaf_v, 4)]
            loads["cl"] = [fetch(cl_hbm, cl, 5)]
        if len(passed) == groups:
            tall = w.shape[0]
            span = dl_hbm.shape[1]
            loads["dl"] = [
                fetch(
                    dl_hbm.at[i * tall : (i + 1) * tall], w.at[:, i * span : (i + 1) * span], 6 + i
                )
                for i in range(2)
            ]

    gathered, quarters, delivered = (ra_0, ra_1), (rq_0, rq_1), (t_0, t_1)

    def view(ra, base, part, third, done, axis, at, half):
        index = []
        lead = True
        split = half is not None
        for name in ("x", "k", "z", "y"):
            if name == "k":
                index.append(k)
            elif name == axis:
                index.append(at)
            elif name in done:
                if split and lead:
                    index.append(pl.ds(2 * half, 2))
                else:
                    index.append(slice(None))
                lead = False
            else:
                index.append(here[name])
        if split and not done:
            index.append(pl.ds(base + half * (third // 2), third // 2))
        else:
            index.append(pl.ds(base, third))
        return ra.at[tuple(index)]

    def program(g):
        lo = g * size
        ra, rq, t = gathered[g], quarters[g], delivered[g]
        rows = slice(lo, lo + size)
        tall = size // 2
        quarter = size // 4

        def root_term(d, h):
            loaded(("w", d, h))
            ids = [chip(ring(a, d), 2 * h + j) for j in range(2)]
            part = jnp.concatenate(
                [w[pl.ds(pl.multiple_of(i * BLOCK, BLOCK), BLOCK), :] for i in ids], axis=0
            )
            return lax.dot_general(root_t[rows, :], part, NT, preferred_element_type=F32)

        halves, used = yield from ring_sum(
            links, root_term, nothing, *first_ring,
            lambda i, h: sa.at[g, i, h, :, :wide], rf1r.at[g], rn1r.at[g],
            lambda i: pool.at[g, i, :, :wide],
        )
        root_done()
        for h in range(2):
            for j in range(2):
                y1[g, 2 * h + j, :, :BLOCK] = halves[h][:, j * BLOCK : (j + 1) * BLOCK]
        block, also = yield from ring_direct(
            links, lambda d: y1[g, ring(b, d), :, :BLOCK], second_ring,
            lambda i: sb.at[g, i, :, :BLOCK], rn2r.at[g],
        )
        used += also
        block = block.astype(BF)
        ra[x, k, z, y] = block
        out_root[rows, :] = block

        orders, third = ("xyz", "yzx", "zxy"), size // 3
        shared = []

        def share(ref):
            shared.append(links(ref, ref, partner))

        moved = []
        for part, order in enumerate(orders):
            own = ra.at[x, k, z, y, pl.ds(part * third, third)]
            moved += [links(own, own, along[order[0]](d)) for d in (2, 1, 3)]
        yield
        if "mid" in loads:
            loaded("mid")
            mid_t[...] = mid_v[...].T
            loaded("leaf")
            leaf_t[...] = leaf_v[...].T
        for copy in moved:
            copy.wait_recv()
        for phase in (1, 2):

            def piece(part, shift_by, half=None):
                order = orders[part]
                axis = order[phase]
                return view(
                    ra, part * third, part, third, order[:phase], axis, ring(here[axis], shift_by), half
                )

            state = []
            for part, order in enumerate(orders):
                own = piece(part, 0)
                axis = order[phase]
                state.append((links(own, own, along[axis](1)), links(own, own, along[axis](3))))
            if phase == 2:
                for part in range(len(orders)):
                    share(piece(part, 0))
            yield
            onward = []
            for part, order in enumerate(orders):
                axis = order[phase]
                state[part][0].wait_recv()
                got = piece(part, 3, 0)
                first = links(got, got, along[axis](1))
                state[part][1].wait_recv()
                got = piece(part, 1, 1)
                onward.append((first, links(got, got, along[axis](3))))
            if phase == 2:
                for part in range(len(orders)):
                    share(piece(part, 3))
                    share(piece(part, 1))
            yield
            for part in range(len(orders)):
                for half in range(2):
                    onward[part][half].wait_recv()
                    if phase == 2:
                        share(piece(part, 2, half))
        yield
        for copy in shared:
            copy.wait_recv()

        def root_block(v):
            return ra[
                lax.div(v, 32), lax.rem(lax.div(v, 16), 2), lax.rem(lax.div(v, 4), 4), lax.rem(v, 4)
            ]

        loaded("c")
        count = bm.shape[1] // 2
        for q in range(count // 16):
            for i in range(4):
                for j in range(4):
                    sp[g, i, :, j * BLOCK : (j + 1) * BLOCK] = root_block(
                        bm[x, k * count + q * 16 + i * 4 + j]
                    )
            left = jnp.concatenate([sp[g, i] for i in range(4)], axis=1)
            term = jnp.dot(
                left, c[q * 16 * BLOCK : (q + 1) * 16 * BLOCK, :], preferred_element_type=F32
            )
            if q == 0:
                pool[g, 0] = term
            else:
                pool[g, 0] += term
        swap = links(pool.at[g, 0], exr.at[g], partner)
        yield
        swap.wait_recv()
        shift[g] = (mid_t[rows, :].astype(F32) - (pool[g, 0] + exr[g])).astype(BF)
        links.sent(used + [swap])
        loaded("dm")

        def mid_term(d, h):
            ids = [chip(ring(a, d), 2 * h + j) for j in range(2)]
            part = jnp.concatenate(
                [dm[pl.ds(pl.multiple_of(i * wide, wide), wide), :] for i in ids], axis=0
            )
            return lax.dot_general(shift[g], part, NT, preferred_element_type=F32)

        halves, used = yield from ring_sum(
            links, mid_term, nothing, *first_ring,
            lambda i, h: sa.at[g, i, h], rf1m.at[g], rn1m.at[g], lambda i: pool.at[g, i],
        )
        for h in range(2):
            for j in range(2):
                y1[g, 2 * h + j] = halves[h][:, j * wide : (j + 1) * wide]
        block, also = yield from ring_direct(
            links, lambda d: y1[g, ring(b, d)], second_ring, lambda i: sb.at[g, i], rn2m.at[g]
        )
        used += also
        block = block.astype(BF)
        out_mid[rows, :] = block
        for i in range(4):
            for j in range(2):
                m4[g, i, j] = block[i * quarter : (i + 1) * quarter, j * BLOCK : (j + 1) * BLOCK]

        moved = []
        for d in (2, 1, 3):
            q = ring(x, d)
            moved.append(links(m4.at[g, q], rq.at[x], (2 * q + k, col)))
        rq[x] = m4[g, x]
        yield
        for copy in moved:
            copy.wait_recv()
        moved = []
        for i, (dz, dy) in enumerate(offsets):
            to = plane(dz, dy)
            ts[g, i] = rq[parents[to]]
            moved.append(links(ts.at[g, i], t.at[k, col], (row, to)))
        t[k, col] = rq[parents[col]]
        shared = [links(t.at[k, col], t.at[k, col], partner)]
        yield
        for copy, (dz, dy) in zip(moved, offsets):
            copy.wait_recv()
            got = t.at[k, plane(4 - dz, 4 - dy)]
            shared.append(links(got, got, partner))
        for copy in shared:
            copy.wait_recv()
        slots = u.shape[2]

        def parent_block(v):
            m = jnp.maximum(v - 128, 0)
            return t[lax.div(m, 32), lax.div(lax.rem(m, 32), 2), lax.rem(m, 2)]

        moved = []
        for d in (2, 1, 3):
            q = ring(x, d)
            for i in range(slots):
                u[g, d - 1, i] = parent_block(bl[col, (2 * q + k) * slots + i])
            moved.append(links(u.at[g, d - 1], bb.at[g, x], (2 * q + k, col)))
        for i in range(slots):
            bb[g, x, i] = parent_block(bl[col, row * slots + i])
        links.sent(used)
        yield
        for copy in moved:
            copy.wait_recv()
        for i in range(slots):
            v = bl[col, row * slots + i]
            side = root_block(jnp.minimum(v, 127)).astype(F32)
            for q in range(4):
                span = slice(q * quarter, (q + 1) * quarter)
                bound[g, span, i * BLOCK : (i + 1) * BLOCK] = jnp.where(
                    v < 128, side[span, :], bb[g, q, i].astype(F32)
                ).astype(BF)

        up, down = along["x"](1), along["x"](3)
        length = shift.shape[2]

        def scatter(product, rp, base, rf, rn):
            out = {}

            def make(d):
                q = ring(x, d)
                sp[g, d] = product(q, 1 - k).astype(BF)
                out[d] = links(sp.at[g, d], rp.at[g, d], partner)
                pool[g, d] = product(q, k)

            def prepare(d):
                if d == 2:
                    make(2)
                    make(1)
                elif d == 1:
                    make(3)
                elif d == 3:
                    make(0)
                out[d].wait_recv()

            def value(d, h):
                span = slice(h * tall, (h + 1) * tall)
                return pool[g, d, span, :] + rp[g, d, span, :].astype(F32)

            halves, used = yield from ring_sum(
                links, value, prepare, up, down,
                lambda i, h: sa.at[g, i, h, base : base + tall], rf.at[g], rn.at[g], None,
            )
            return halves, list(out.values())

        loaded("cl")
        halves, used = yield from scatter(
            lambda q, core: jnp.dot(
                bound[g],
                cl[:, pl.ds(pl.multiple_of((2 * q + core) * length, length), length)],
                preferred_element_type=F32,
            ),
            rp1, 0, rf1l, rn1l,
        )
        for h in range(2):
            shift[g, h * tall : (h + 1) * tall, :] = (
                leaf_t[lo + h * tall : lo + (h + 1) * tall, :].astype(F32) - halves[h]
            ).astype(BF)
        links.sent(used)
        loaded("dl")
        halves, used = yield from scatter(
            lambda q, core: lax.dot_general(
                shift[g],
                w[
                    pl.ds(pl.multiple_of((2 * lax.rem(q, 2) + core) * length, length), length),
                    pl.ds(pl.multiple_of(lax.div(q, 2) * length, length), length),
                ],
                NT,
                preferred_element_type=F32,
            ),
            rp2, tall, rf2l, rn2l,
        )
        for h in range(2):
            out_leaf[lo + h * tall : lo + (h + 1) * tall, :] = halves[h].astype(BF)

    together([program(g) for g in range(groups)], lag)
    links.drain()
    assert len(links.made) == send.shape[0], len(links.made)


def turned(*refs):
    half = len(refs) // 2
    for source, target in zip(refs[:half], refs[half:]):
        target[...] = source[...].T


VM = pl.BlockSpec(memory_space=pltpu.VMEM)
SM = pl.BlockSpec(memory_space=pltpu.SMEM)
ANY = pl.BlockSpec(memory_space=pl.ANY)
GROUPS = 2
COPIES = 124
LAG = 0


def shards(
    dinv_root, rhs_root, dinv_mid, coup_mid, rhs_mid, dinv_leaf, coup_leaf, rhs_leaf,
    bounds_mid, bounds_leaf, parents,
):
    n = rhs_root.shape[1]
    slots = bounds_leaf.shape[1] // 8
    wide = 2 * BLOCK
    length = rhs_leaf.shape[1]
    g, r = GROUPS, n // GROUPS
    scratch = [
        (rhs_root.shape, BF), (rhs_root.shape[::-1], BF),
        (rhs_mid.shape[1:], BF), ((n, length), BF), (rhs_leaf.shape[1:], BF), ((n, length), BF),
        (dinv_root.shape, BF), (coup_mid.shape, BF), (dinv_mid.shape, BF), (coup_leaf.shape[1:], BF),
        ((4, 2, 4, 4, r, BLOCK), BF), ((4, 2, 4, 4, r, BLOCK), BF),
        ((g, 4, r, length), F32), ((g, 4, r, wide), F32),
        ((g, 3, 2, r, length), BF), ((g, 3, r, wide), BF),
        ((g, 2, r, wide), BF), ((g, 2, 2, r, wide), BF),
        ((g, 3, r, BLOCK), BF),
        ((g, 2, r, length), BF), ((g, 2, 2, r, length), BF),
        ((g, 3, r, wide), BF),
        ((g, r, length), F32), ((g, r, length), BF),
        ((g, 4, 2, r // 4, BLOCK), BF), ((4, 2, r // 4, BLOCK), BF), ((4, 2, r // 4, BLOCK), BF),
        ((g, 15, 2, r // 4, BLOCK), BF), ((2, 16, 2, r // 4, BLOCK), BF), ((2, 16, 2, r // 4, BLOCK), BF),
        ((g, 3, slots, r // 4, BLOCK), BF), ((g, 4, slots, r // 4, BLOCK), BF),
        ((g, r, slots * BLOCK), BF),
        ((g, 4, r, length), BF), ((g, 4, r, length), BF), ((g, 4, r, length), BF),
        ((g, 2, r // 2, length), BF), ((g, 2, 2, r // 2, length), BF),
        ((g, 2, r // 2, length), BF), ((g, 2, 2, r // 2, length), BF),
    ]
    copies = COPIES * g
    outs = pl.pallas_call(
        functools.partial(kernel, GROUPS, LAG),
        out_shape=tuple(jax.ShapeDtypeStruct((n, width), BF) for width in (BLOCK, wide, length)),
        in_specs=[SM] * 3 + [ANY] * 8,
        out_specs=(VM,) * 3,
        scratch_shapes=[pltpu.VMEM(shape, kind) for shape, kind in scratch]
        + [
            pltpu.SemaphoreType.DMA((24,)),
            pltpu.SemaphoreType.DMA((copies,)),
            pltpu.SemaphoreType.DMA((copies,)),
        ],
        compiler_params=pltpu.CompilerParams(
            collective_id=0, has_side_effects=True, vmem_limit_bytes=67043328
        ),
    )(
        bounds_mid, bounds_leaf, parents, rhs_root, rhs_mid, rhs_leaf[0],
        dinv_root, coup_mid, dinv_mid, coup_leaf[0], dinv_leaf[0],
    )
    root, mid, leaf = pl.pallas_call(
        turned,
        out_shape=tuple(jax.ShapeDtypeStruct(out.shape[::-1], BF) for out in outs),
        in_specs=[VM] * 3,
        out_specs=(VM,) * 3,
    )(*outs)
    return root, mid, leaf[None]


def solution(mesh):
    return jax.shard_map(
        shards,
        mesh=mesh,
        in_specs=(
            P("row", "col"),
            P("col", None),
            P("row", "col"),
            P("row", "col"),
            P(None, "col", None),
            P("col", None, "row"),
            P("col", "row", None),
            P("col", "row", None),
            P(),
            P(),
            P(),
        ),
        out_specs=(P(("row", "col"), None), P(("row", "col"), None), P("col", "row", None)),
        check_vma=False,
    )
```
